32 devices in a mesh: dom: 8 (over z, x), rep: 4 (over y, core).
Axes of the slice: x: 2, y: 2, z: 4, core: 2. Of those that a mesh axis runs over, the one named last changes fastest.
Arguments:
- elem_rows: bfloat16 [65536, 512], P(('dom', 'rep')), may hold values from -6 to 6
- elem_block: int32 [65536], P(('dom', 'rep')), may hold values from 0 to 3
- send_lists: int32 [65536], P(('dom', 'rep')), may hold values from 0 to 2047, as said below
- halo_block: int32 [65536], P(('dom', 'rep')), may hold values from 0 to 3
- born_rows: bfloat16 [2048, 512], P(('dom', 'rep')), may hold values from -6 to 6
- born_owner: int32 [2048, 1], P(('dom', 'rep')), may hold values from 0 to 31; in each aligned block of 64 rows (0 to 63, 64 to 127, ...) at most 4 rows name the same one
- mass: float32 [16384], P(('dom', 'rep')), may hold values from 0.5 to 4
Outputs:
- factor: float32 [16384, 512], P(('dom', 'rep'))
The draws below stay inside these ranges and needn't reach their ends.
Inputs may be any that keep to these rules, and one draw needn't show every extreme that they name: `send_lists`: each half of one device's list names 1024 distinct rows of that device. `born_owner`: among the born rows of one device at most 4 name the same owner.
All inputs are finite; a program needn't handle non-finite values.
Results may differ from the reference program's by a relative error of at most 0.0003.
Values may be sent and summed in bfloat16 or wider, within the bound.
A program may use at most 64 MiB of HBM per device.

```python
import math
import jax
import jax.numpy as jnp
import numpy as np
from jax import lax

W = 512
E_DEV = 2048
H = 1024
CAP = 4
NBLK = 32
BORN_DEV = 64
N_DOM = 8
N_REP = 4


def draw_send_lists(key, part):
    device_keys = jax.random.split(jax.random.fold_in(key, 17), NBLK * 2)

    def one_half(half_key):
        return jax.random.permutation(half_key, E_DEV)[:H]
    chosen = jax.vmap(one_half)(device_keys)
    return chosen.reshape(-1).astype(jnp.int32)


def touch_ends(values, key, smallest, high):
    longest = values.shape.index(max(values.shape))
    spots = []
    for shift in (0, 1):
        where = [jax.random.randint(jax.random.fold_in(key, axis), (), 0, length) for axis, length in enumerate(values.shape)]
        where[longest] = (where[longest] + shift) % values.shape[longest]
        spots.append(tuple(where))
    return values.at[spots[0]].set(smallest).at[spots[1]].set(high)


def block_scale(key, dims, cuts, low, top_value):
    level = 1.0
    for dim, blocks in cuts:
        heights = jax.random.uniform(jax.random.fold_in(jax.random.fold_in(key, 6), dim), (blocks,), jnp.float32, low / len(cuts), top_value / len(cuts))
        level = level * jnp.repeat(jnp.exp(heights), dims[dim] // blocks).reshape((-1,) + (1,) * (len(dims) - 1 - dim))
    return level


def assign_block(key, own, number, rows, amount, top, bound, skew):
    ranking = jax.random.permutation(key, amount)
    packed, common = portions_of(amount, rows * top, bound, skew, True), portions_of(amount, rows * top, bound, skew, False)
    places = jnp.arange(amount)

    def named(tallies, offset_by):
        used = int((tallies > 0).sum())
        fixed = max(1, used // 4)
        passed = fixed + (places - fixed + offset_by * (used - fixed)) % max(1, amount - fixed)
        return jnp.zeros((amount,), jnp.int32).at[ranking[jnp.where(places < fixed, places, passed)]].set(jnp.asarray(tallies, jnp.int32))

    tallies = jnp.where(number % 4 == 0, named(packed, number // 4), named(common, number - number // 4 - 1))
    mixed = jax.random.permutation(jax.random.fold_in(own, 3), amount)
    donor, taker = mixed[0:amount // 2 * 2:2], mixed[1:amount // 2 * 2:2]
    room = jnp.minimum(tallies[donor] - 1, bound - tallies[taker]) // 2
    room = jnp.where((donor == ranking[0]) | (taker == ranking[0]) | (tallies[taker] == 0), 0, jnp.maximum(room, 0))
    passed = jax.random.randint(jax.random.fold_in(own, 4), (amount // 2,), 0, 1 << 20) % (room + 1)
    tallies = tallies.at[donor].add(-passed).at[taker].add(passed)
    members = jnp.searchsorted(jnp.cumsum(tallies), jnp.arange(rows * top), side="right").astype(jnp.int32)
    table = members.reshape(top, rows).T
    table = table[jax.random.permutation(jax.random.fold_in(own, 1), rows)]
    offset_by = jax.random.randint(jax.random.fold_in(own, 2), (rows, 1), 0, top)
    return jnp.take_along_axis(table, (jnp.arange(top)[None, :] + offset_by) % top, axis=1)


def portions_of(number_of, total, bound, slope, full):
    weights = [(1 << 20) // math.isqrt(rank ** slope) + 1 for rank in range(1, number_of + 1)]
    largest = bound if full else min(bound, max(-(-total // number_of), total * weights[0] // sum(weights)))
    least = 1 if total - largest >= number_of - 1 else 0
    holding, spare = [largest] + [least] * (number_of - 1), total - largest - least * (number_of - 1)
    while spare > 0:
        free = [i for i in range(1, number_of) if holding[i] < largest] or [i for i in range(1, number_of) if holding[i] < bound]
        pool, left = sum([weights[i] for i in free]), spare
        for i in free:
            extra = min(bound - holding[i], max(1, left * weights[i] // pool), spare)
            holding[i] = holding[i] + extra
            spare = spare - extra
    return np.array(holding)


def normal_values(key, shape, deviation, limit, cuts=(), held_as=jnp.bfloat16):
    result = jax.random.normal(key, shape, jnp.float32) * deviation
    if len(cuts) > 0:
        result = block_scale(key, shape, cuts, -0.22, 0.18) * result
    return jnp.clip(result, min=-limit, max=limit).astype(held_as)


def setup_inputs(seed: int = 0) -> dict:
    streams_of = jax.random.split(jax.random.key(seed), 8)
    elem_rows = normal_values(streams_of[0], (NBLK * E_DEV, W), 1.0, 6.0, ((0, 32),))
    elem_block = touch_ends(jax.random.randint(streams_of[1], (NBLK * E_DEV,), 0, N_REP), jax.random.fold_in(streams_of[1], 1), 0, N_REP - 1).astype(jnp.int32)
    send_lists = draw_send_lists(jax.random.fold_in(streams_of[7], 71), 0)
    halo_block = touch_ends(jax.random.randint(streams_of[3], (NBLK * 2 * H,), 0, N_REP), jax.random.fold_in(streams_of[3], 1), 0, N_REP - 1).astype(jnp.int32)
    born_rows = normal_values(streams_of[4], (NBLK * BORN_DEV, W), 1.0, 6.0, ((0, 32),))
    born_owner_keys = jax.random.split(jax.random.fold_in(streams_of[5], 1), (NBLK * BORN_DEV) // BORN_DEV)
    born_owner_turns = jax.random.permutation(jax.random.fold_in(streams_of[5], 3), (NBLK * BORN_DEV) // BORN_DEV)
    born_owner = jax.vmap(lambda own, number: assign_block(jax.random.fold_in(streams_of[5], 2), own, number, BORN_DEV, NBLK, 1, CAP, 2))(born_owner_keys, born_owner_turns).reshape((NBLK * BORN_DEV, 1))
    mass = jnp.clip(0.5 + 3.5 * jax.random.uniform(streams_of[6], (NBLK * W,), jnp.float32) ** block_scale(streams_of[6], (NBLK * W,), ((0, 32),), -0.2, 0.2), 0.5, 4.0)
    return {"elem_rows": elem_rows, "elem_block": elem_block, "send_lists": send_lists, "halo_block": halo_block, "born_rows": born_rows, "born_owner": born_owner, "mass": mass}


def pick_rows(row_data, chosen):
    return jnp.take(row_data, chosen, axis=0)

def reference(elem_rows, elem_block, send_lists, halo_block, born_rows, born_owner, mass):
    rows_dev = elem_rows.reshape(NBLK, E_DEV, W)
    list_pairs = send_lists.reshape(NBLK, 2 * H)
    listed_rows = jax.vmap(pick_rows)(rows_dev, list_pairs).reshape(N_DOM, N_REP, 2, H, W)
    to_lower = listed_rows[:, :, 0]
    to_upper = listed_rows[:, :, 1]
    empty_part = jnp.zeros((1, N_REP, H, W), jnp.bfloat16)
    from_lower = jnp.concatenate([empty_part, to_upper[:-1]], axis=0)
    from_upper = jnp.concatenate([to_lower[1:], empty_part], axis=0)
    halo_rows = jnp.concatenate([from_lower, from_upper], axis=2).reshape(N_DOM, N_REP * 2 * H, W)
    halo_ids = halo_block.reshape(N_DOM, N_REP * 2 * H)
    own_rows = elem_rows.reshape(N_DOM, N_REP * E_DEV, W)
    own_ids = elem_block.reshape(N_DOM, N_REP * E_DEV)
    row_pool = jnp.concatenate([own_rows, halo_rows], axis=1)
    pool_ids = jnp.concatenate([own_ids, halo_ids], axis=1)
    owner_codes = born_owner[:, 0]
    sorted_order = jnp.argsort(owner_codes, stable=True)
    window = NBLK * CAP
    sorted_rows = jnp.concatenate([born_rows[sorted_order], jnp.zeros((window, W), jnp.bfloat16)], axis=0)
    owner_counts = jax.ops.segment_sum(jnp.ones_like(owner_codes), owner_codes, NBLK).astype(jnp.int32)
    offsets = (jnp.cumsum(owner_counts) - owner_counts).astype(jnp.int32)
    mass_blocks = mass.reshape(NBLK, W)

    def factor_block(block_index):
        partition = block_index // N_REP
        block_id = block_index % N_REP
        row_data = row_pool[partition]
        in_block = pool_ids[partition] == block_id
        masked = jnp.where(in_block[:, None], row_data, jnp.zeros((), jnp.bfloat16))
        block_gram = jnp.dot(masked.T.astype(jnp.float32), row_data.astype(jnp.float32), preferred_element_type=jnp.float32)
        window_rows = lax.dynamic_slice_in_dim(sorted_rows, offsets[block_index].astype(jnp.int32), window, 0)
        live_rows = jnp.arange(window, dtype=jnp.int32) < owner_counts[block_index]
        born_masked = jnp.where(live_rows[:, None], window_rows, jnp.zeros((), jnp.bfloat16))
        block_gram = block_gram + jnp.dot(born_masked.T.astype(jnp.float32), window_rows.astype(jnp.float32), preferred_element_type=jnp.float32)
        system = jnp.diag(mass_blocks[block_index]) + block_gram / W
        return jnp.linalg.cholesky(system)
    factors = lax.map(factor_block, jnp.arange(NBLK, dtype=jnp.int32))
    return factors.reshape(NBLK * W, W)
```

```python
import jax
import jax.numpy as jnp
from jax import lax
from jax.experimental import pallas as pl
from jax.experimental.pallas import tpu as pltpu
from jax.sharding import PartitionSpec as P

F=jnp.float32; BF=jnp.bfloat16

def split3(v):
    hi=v.astype(BF); r=v-hi.astype(F); mid=r.astype(BF); lo=(r-mid.astype(F)).astype(BF)
    return hi,mid,lo

def chol_kernel(S, out, A, nt):
    n=S.shape[0]; nb=128; st=8
    S0=S
    for k in range(n//nb):
        o=k*nb
        r_i=lax.broadcasted_iota(jnp.int32,(nb,nb),0); c_i=lax.broadcasted_iota(jnp.int32,(nb,nb),1)
        A[:, :nb]=S[o:o+nb,o:o+nb]
        A[:, nb:]=jnp.where(r_i==c_i,1.0,0.0)
        sub=lax.broadcasted_iota(jnp.int32,(st,nb),0)
        for s in range(nb//st):
            a=s*st
            TA=A[a:a+st,:nb]; TW=A[a:a+st,nb:]
            B=[jnp.broadcast_to(TA[:,a+c:a+c+1],(st,nb)) for c in range(st)]
            D=jnp.zeros((st,nb),F)
            for c in range(st):
                piv=jnp.broadcast_to(B[c][c:c+1,:],(st,nb))
                D=jnp.where(sub==c,piv,D)
                if c<st-1:
                    m=jnp.where(sub>c,B[c]/piv,0.0)
                    for e in range(c+1,st):
                        B[e]=B[e]-m*B[e][c:c+1,:]
                    TA=TA-m*TA[c:c+1,:]
                    TW=TW-m*TW[c:c+1,:]
            q=lax.rsqrt(D)
            VA=TA*q; VW=TW*q
            A[a:a+st,:nb]=VA; A[a:a+st,nb:]=VW
            if s<nb//st-1:
                V=jnp.concatenate([VA,VW],axis=1)
                hi,mid,lo=split3(V)
                hi=hi.astype(F);mid=mid.astype(F);lo=lo.astype(F)
                L=jnp.concatenate([hi,hi,mid,hi,mid,lo],axis=0)[:,:nb].T.astype(BF)
                R=jnp.concatenate([hi,mid,hi,lo,mid,hi],axis=0).astype(BF)
                b=a+st
                A[b:,:]=A[b:,:]-lax.dot_general(L,R,(((1,),(0,)),((),())),preferred_element_type=F)[b:,:]
        out[o:o+nb,o:o+nb]=jnp.where(c_i<=r_i,A[:,:nb].T,0.0)
        if k<n//nb-1:
            out[o:o+nb,o+nb:]=jnp.zeros((nb,n-o-nb),F)
            W=jnp.where(c_i<=r_i,A[:,nb:],0.0)
            L21=lax.dot_general(S[o+nb:,o:o+nb],W,(((1,),(1,)),((),())),precision=lax.Precision.HIGHEST,preferred_element_type=F)
            out[o+nb:,o:o+nb]=L21
            S[o+nb:,o+nb:]=S[o+nb:,o+nb:]-lax.dot_general(L21,L21,(((1,),(1,)),((),())),precision=lax.Precision.HIGHEST,preferred_element_type=F)

def chol(s):
    n=s.shape[0]
    def body(si,out,S,A):
        S[...]=si[...]
        chol_kernel(S,out,A,None)
    return pl.pallas_call(body,out_shape=jax.ShapeDtypeStruct((n,n),F),
        in_specs=[pl.BlockSpec(memory_space=pltpu.VMEM)],out_specs=pl.BlockSpec(memory_space=pltpu.VMEM),
        scratch_shapes=[pltpu.VMEM((n,n),F),pltpu.VMEM((128,256),F)])(s)


CAP = 4


def with_halo(value, sides, width):
    for axis, dim in sides:
        devices, length = (lax.axis_size(axis), value.shape[dim])
        up = [(i, (i + 1) % devices) for i in range(devices - 1)]
        down = [(j, i) for i, j in up]
        last = lax.slice_in_dim(value, length - width, length, axis=dim)
        leading = lax.slice_in_dim(value, 0, width, axis=dim)
        before = lax.ppermute(last, axis, up)
        after = lax.ppermute(leading, axis, down)
        value = jnp.concatenate([before, value, after], axis=dim)
    return value


def local(elem_rows, elem_block, send_lists, halo_block, born_rows, born_owner, mass):
    width = elem_rows.shape[1]
    dom_size = lax.axis_size("dom")
    rep_size = lax.axis_size("rep")
    list_half = send_lists.shape[0] // 2
    listed = jnp.take(elem_rows, send_lists, axis=0)
    padded = with_halo(listed, (("dom", 0),), list_half)
    halo_rows = jnp.concatenate([padded[:list_half], padded[3 * list_half :]], axis=0)
    born_count = born_rows.shape[0]
    slot_total = dom_size * rep_size
    owner_codes = born_owner[:, 0]
    onehot = (owner_codes[:, None] == jnp.arange(slot_total, dtype=jnp.int32)[None, :]).astype(
        jnp.bfloat16
    )
    row_index = jnp.arange(born_count, dtype=jnp.int32)
    earlier = (row_index[None, :] < row_index[:, None]).astype(jnp.bfloat16)
    counts = jnp.dot(earlier, onehot, preferred_element_type=jnp.float32)
    slot_rank = jnp.sum(counts * onehot.astype(jnp.float32), axis=1).astype(jnp.int32)
    position = owner_codes * CAP + slot_rank
    packed = jnp.zeros((slot_total * CAP, width), jnp.bfloat16).at[position].set(born_rows)
    packed_four = packed.reshape(dom_size, rep_size, CAP, width)
    arrived = lax.all_to_all(
        lax.all_to_all(packed_four, "dom", split_axis=0, concat_axis=0, tiled=True),
        "rep",
        split_axis=1,
        concat_axis=1,
        tiled=True,
    )
    born_pool = arrived.reshape(-1, width)
    row_pool = jnp.concatenate([elem_rows, halo_rows], axis=0)
    pool_block = jnp.concatenate([elem_block, halo_block], axis=0)
    owner_gram = lax.dot_general(
        born_pool, born_pool, (((0,), (0,)), ((), ())), preferred_element_type=jnp.float32
    )
    stacked = jnp.concatenate(
        [
            row_pool * (pool_block == block_id)[:, None].astype(jnp.bfloat16)
            for block_id in range(rep_size)
        ],
        axis=1,
    )
    block_gram = lax.psum_scatter(
        lax.dot_general(
            stacked, row_pool, (((0,), (0,)), ((), ())), preferred_element_type=jnp.float32
        ),
        "rep",
        scatter_dimension=0,
        tiled=True,
    )
    block_gram = block_gram + owner_gram
    system = jnp.diag(mass) + block_gram / width
    return chol(system)


def solution(mesh):
    in_specs = (
        P(("dom", "rep"), None),
        P(("dom", "rep")),
        P(("dom", "rep")),
        P(("dom", "rep")),
        P(("dom", "rep"), None),
        P(("dom", "rep"), None),
        P(("dom", "rep")),
    )
    out_specs = P(("dom", "rep"), None)
    return jax.shard_map(local, mesh=mesh, in_specs=in_specs, out_specs=out_specs, check_vma=False)
```

```python
import functools

import jax
import jax.numpy as jnp
from jax import lax
from jax.experimental import pallas as pl
from jax.experimental.pallas import tpu as pltpu
from jax.sharding import PartitionSpec as P

CAP = 4
F=jnp.float32; BF=jnp.bfloat16

def split3(v):
    hi=v.astype(BF); r=v-hi.astype(F); mid=r.astype(BF); lo=(r-mid.astype(F)).astype(BF)
    return hi,mid,lo

def chol_kernel(S, out, A):
    n=S.shape[0]; nb=128; st=8
    for k in range(n//nb):
        o=k*nb
        r_i=lax.broadcasted_iota(jnp.int32,(nb,nb),0); c_i=lax.broadcasted_iota(jnp.int32,(nb,nb),1)
        A[:, :nb]=S[o:o+nb,o:o+nb]
        A[:, nb:]=jnp.where(r_i==c_i,1.0,0.0)
        sub=lax.broadcasted_iota(jnp.int32,(st,nb),0)
        for s in range(nb//st):
            a=s*st
            TA=A[a:a+st,:nb]; TW=A[a:a+st,nb:]
            B=[jnp.broadcast_to(TA[:,a+c:a+c+1],(st,nb)) for c in range(st)]
            D=jnp.zeros((st,nb),F)
            for c in range(st):
                piv=jnp.broadcast_to(B[c][c:c+1,:],(st,nb))
                D=jnp.where(sub==c,piv,D)
                if c<st-1:
                    m=jnp.where(sub>c,B[c]/piv,0.0)
                    for e in range(c+1,st):
                        B[e]=B[e]-m*B[e][c:c+1,:]
                    TA=TA-m*TA[c:c+1,:]
                    TW=TW-m*TW[c:c+1,:]
            q=lax.rsqrt(D)
            VA=TA*q; VW=TW*q
            A[a:a+st,:nb]=VA; A[a:a+st,nb:]=VW
            if s<nb//st-1:
                V=jnp.concatenate([VA,VW],axis=1)
                hi,mid,lo=split3(V)
                hi=hi.astype(F);mid=mid.astype(F);lo=lo.astype(F)
                L=jnp.concatenate([hi,hi,mid,hi,mid,lo],axis=0)[:,:nb].T.astype(BF)
                R=jnp.concatenate([hi,mid,hi,lo,mid,hi],axis=0).astype(BF)
                b=a+st
                A[b:,:]=A[b:,:]-lax.dot_general(L,R,(((1,),(0,)),((),())),preferred_element_type=F)[b:,:]
        out[o:o+nb,o:o+nb]=jnp.where(c_i<=r_i,A[:,:nb].T,0.0)
        if k<n//nb-1:
            out[o:o+nb,o+nb:]=jnp.zeros((nb,n-o-nb),F)
            W=jnp.where(c_i<=r_i,A[:,nb:],0.0)
            L21=lax.dot_general(S[o+nb:,o:o+nb],W,(((1,),(1,)),((),())),precision=lax.Precision.HIGHEST,preferred_element_type=F)
            out[o+nb:,o:o+nb]=L21
            S[o+nb:,o+nb:]=S[o+nb:,o+nb:]-lax.dot_general(L21,L21,(((1,),(1,)),((),())),precision=lax.Precision.HIGHEST,preferred_element_type=F)

CH = 256


def gram_add(G, b, T, R, ids):
    width = R.shape[1]
    M = jnp.where(ids == b, T, jnp.zeros((), T.dtype))
    at = 0
    for j in range(width // 256):
        o = 256 * j
        p = jnp.dot(M[o:, :], R[:, o : o + 256], preferred_element_type=F)
        h = width - o
        G[b, at : at + h, :] += p[:, :128]
        G[b, at + h : at + 2 * h - 128, :] += p[128:, 128:]
        at += 2 * h - 128


def exchange_kernel(doms, reps, cap, rows, eblk, lists, hblk, born, own_c, own_r, out,
                    TR, sbuf, rbuf, G, RB, bpack, brecv,
                    ssem, rsem, bss, brs, xss, xrs, lsem):
    p = lax.axis_index("dom")
    q = lax.axis_index("rep")
    me = p * reps + q
    total = doms * reps
    n_rows, width = rows.shape
    nch = sbuf.shape[1]
    cols = width // 128
    slab = cap * cols

    def halo_copy(d, ch):
        return pltpu.make_async_remote_copy(
            src_ref=sbuf.at[d, ch], dst_ref=rbuf.at[1 - d, ch],
            send_sem=ssem.at[d, ch], recv_sem=rsem.at[1 - d, ch],
            device_id={"dom": p + 2 * d - 1, "rep": q}, device_id_type=pl.DeviceIdType.MESH)

    def halo_wait(slot, ch):
        return pltpu.make_async_remote_copy(
            src_ref=sbuf.at[slot, ch], dst_ref=rbuf.at[slot, ch],
            send_sem=ssem.at[slot, ch], recv_sem=rsem.at[slot, ch],
            device_id={"dom": p + 2 * slot - 1, "rep": q}, device_id_type=pl.DeviceIdType.MESH)

    exists = (p > 0, p < doms - 1)

    for c in range(n_rows // CH):
        TR[:, c * CH : (c + 1) * CH] = rows[c * CH : (c + 1) * CH, :].T

    def gather_step(ch, _):
        for d in range(2):
            @pl.when(exists[d])
            def _():
                l = lists[:, pl.ds(pl.multiple_of((d * nch + ch) * CH, CH), CH)]
                i = lax.broadcasted_iota(jnp.int32, (n_rows, CH), 0)
                PT = jnp.where(i == l, 1.0, 0.0).astype(BF)
                sbuf[d, ch] = jnp.dot(TR[...], PT, preferred_element_type=F).astype(BF)
                halo_copy(d, ch).start()
        return 0

    lax.fori_loop(0, nch, gather_step, 0)

    n_born = born.shape[0]
    ii = lax.broadcasted_iota(jnp.int32, (n_born, n_born), 0)
    jj = lax.broadcasted_iota(jnp.int32, (n_born, n_born), 1)
    same = (own_c[...] == own_r[...]) & (ii < jj)
    rank = jnp.sum(jnp.where(same, 1.0, 0.0), axis=0, keepdims=True).astype(jnp.int32)
    base = own_r[...] * slab + rank * cols
    m = lax.broadcasted_iota(jnp.int32, (total * slab, n_born), 0)
    acc = jnp.zeros((total * slab, 128), F)
    for c in range(cols):
        oh = jnp.where(m == base + c, 1.0, 0.0).astype(BF)
        acc += jnp.dot(oh, born[:, c * 128 : (c + 1) * 128], preferred_element_type=F)
    bpack[...] = acc.astype(BF)

    def born_copy(to, frm):
        return pltpu.make_async_remote_copy(
            src_ref=bpack.at[pl.ds(pl.multiple_of(to * slab, slab), slab), :],
            dst_ref=brecv.at[pl.ds(pl.multiple_of(frm * slab, slab), slab), :],
            send_sem=bss.at[to], recv_sem=brs.at[frm],
            device_id={"dom": to // reps, "rep": to % reps}, device_id_type=pl.DeviceIdType.MESH)

    def born_send(k, _):
        to = (me + k) % total
        born_copy(to, me).start()
        return 0

    lax.fori_loop(1, total, born_send, 0)
    mine = pl.ds(pl.multiple_of(me * slab, slab), slab)
    local = pltpu.make_async_copy(bpack.at[mine, :], brecv.at[mine, :], lsem)
    local.start()

    G[...] = jnp.zeros_like(G)

    def own_step(c, _):
        at = pl.ds(pl.multiple_of(c * CH, CH), CH)
        T = TR[:, at]
        R = rows[at, :]
        ids = eblk[:, at]

        def one(b, _):
            gram_add(G, b, T, R, ids)
            return 0
        lax.fori_loop(0, reps, one, 0)
        return 0

    lax.fori_loop(0, n_rows // CH, own_step, 0)

    def halo_step(ch, _):
        for slot in range(2):
            @pl.when(exists[slot])
            def _():
                halo_wait(slot, ch).wait_recv()
                T = rbuf[slot, ch]
                R = T.T
                ids = hblk[:, pl.ds(pl.multiple_of((slot * nch + ch) * CH, CH), CH)]

                def one(b, _):
                    gram_add(G, b, T, R, ids)
                    return 0
                lax.fori_loop(0, reps, one, 0)
        return 0

    lax.fori_loop(0, nch, halo_step, 0)

    sent = []
    step, slot = 1, 0
    while step < reps:
        bit = (q // step) % 2
        peer = q + step * (1 - 2 * bit)
        low = q % step
        copies = []
        for i in range(reps // (2 * step)):
            away = low + (1 - bit) * step + 2 * step * i
            cp = pltpu.make_async_remote_copy(
                src_ref=G.at[away], dst_ref=RB.at[slot + i],
                send_sem=xss.at[slot + i], recv_sem=xrs.at[slot + i],
                device_id={"dom": p, "rep": peer}, device_id_type=pl.DeviceIdType.MESH)
            cp.start()
            copies.append(cp)
        for i, cp in enumerate(copies):
            keep = low + bit * step + 2 * step * i
            cp.wait_recv()
            G[keep] += RB[slot + i]
        sent += copies
        slot += len(copies)
        step *= 2

    def born_wait(k, _):
        frm = (me + k) % total
        born_copy(frm, frm).wait_recv()
        return 0

    lax.fori_loop(1, total, born_wait, 0)
    local.wait()
    n = total * cap
    mm = lax.broadcasted_iota(jnp.int32, (n, total * slab), 0)
    kk = lax.broadcasted_iota(jnp.int32, (n, total * slab), 1)
    Bv = brecv[...]
    V = jnp.concatenate(
        [jnp.dot(jnp.where(kk == mm * cols + c, 1.0, 0.0).astype(BF), Bv, preferred_element_type=F)
         for c in range(cols)], axis=1)
    VT = V.T.astype(BF)
    V = V.astype(BF)
    at = 0
    for j in range(width // 128):
        h = width - 128 * j
        out[at : at + h, :] = G[q, at : at + h, :] + jnp.dot(
            VT[128 * j :, :], V[:, 128 * j : 128 * j + 128], preferred_element_type=F)
        at += h

    for cp in sent:
        cp.wait_send()

    def born_done(k, _):
        to = (me + k) % total
        born_copy(to, me).wait_send()
        return 0

    lax.fori_loop(1, total, born_done, 0)

    def halo_done(ch, _):
        for d in range(2):
            @pl.when(exists[d])
            def _():
                halo_copy(d, ch).wait_send()
        return 0

    lax.fori_loop(0, nch, halo_done, 0)


def factor_kernel(packed, mass, out, S, A):
    width = S.shape[0]
    r_i = lax.broadcasted_iota(jnp.int32, (128, 128), 0)
    c_i = lax.broadcasted_iota(jnp.int32, (128, 128), 1)
    at = 0
    for j in range(width // 128):
        o = 128 * j
        h = width - o
        S[o:, o : o + 128] = packed[at : at + h, :] / width
        S[o : o + 128, o : o + 128] += jnp.where(r_i == c_i, mass[:, o : o + 128], 0.0)
        at += h
    chol_kernel(S, out, A)


def solution(mesh):
    doms, reps = mesh.shape["dom"], mesh.shape["rep"]
    total = doms * reps

    def local(elem_rows, elem_block, send_lists, halo_block, born_rows, born_owner, mass):
        n_rows, width = elem_rows.shape
        nch = send_lists.shape[0] // 2 // CH
        tri = (width // 128) * (width // 128 + 1) // 2 * 128
        slab = CAP * (width // 128)
        vm = pl.BlockSpec(memory_space=pltpu.VMEM)
        packed = pl.pallas_call(
            functools.partial(exchange_kernel, doms, reps, CAP),
            out_shape=jax.ShapeDtypeStruct((tri, 128), F),
            in_specs=[vm] * 7,
            out_specs=vm,
            scratch_shapes=[
                pltpu.VMEM((width, n_rows), BF),
                pltpu.VMEM((2, nch, width, CH), BF),
                pltpu.VMEM((2, nch, width, CH), BF),
                pltpu.VMEM((reps, tri, 128), F),
                pltpu.VMEM((reps - 1, tri, 128), F),
                pltpu.VMEM((total * slab, 128), BF),
                pltpu.VMEM((total * slab, 128), BF),
                pltpu.SemaphoreType.DMA((2, nch)),
                pltpu.SemaphoreType.DMA((2, nch)),
                pltpu.SemaphoreType.DMA((total,)),
                pltpu.SemaphoreType.DMA((total,)),
                pltpu.SemaphoreType.DMA((reps - 1,)),
                pltpu.SemaphoreType.DMA((reps - 1,)),
                pltpu.SemaphoreType.DMA,
            ],
            compiler_params=pltpu.CompilerParams(has_side_effects=True),
        )(elem_rows, elem_block[None, :], send_lists[None, :], halo_block[None, :],
          born_rows, born_owner, born_owner.reshape(1, -1))
        return pl.pallas_call(
            factor_kernel,
            out_shape=jax.ShapeDtypeStruct((width, width), F),
            in_specs=[vm] * 2,
            out_specs=vm,
            scratch_shapes=[pltpu.VMEM((width, width), F), pltpu.VMEM((128, 256), F)],
        )(packed, mass[None, :])

    both = P(("dom", "rep"))
    rows2 = P(("dom", "rep"), None)
    return jax.shard_map(local, mesh=mesh, in_specs=(rows2, both, both, both, rows2, rows2, both),
                         out_specs=rows2, check_vma=False)
```

```python
import functools

import jax
import jax.numpy as jnp
from jax import lax
from jax.experimental import pallas as pl
from jax.experimental.pallas import tpu as pltpu
from jax.sharding import PartitionSpec as P

CAP = 4
F=jnp.float32; BF=jnp.bfloat16

def split3(v):
    hi=v.astype(BF); r=v-hi.astype(F); mid=r.astype(BF); lo=(r-mid.astype(F)).astype(BF)
    return hi,mid,lo

def chol_kernel(S, out, A):
    n=S.shape[0]; nb=128; st=8
    for k in range(n//nb):
        o=k*nb
        r_i=lax.broadcasted_iota(jnp.int32,(nb,nb),0); c_i=lax.broadcasted_iota(jnp.int32,(nb,nb),1)
        A[:, :nb]=S[o:o+nb,o:o+nb]
        A[:, nb:]=jnp.where(r_i==c_i,1.0,0.0)
        sub=lax.broadcasted_iota(jnp.int32,(st,nb),0)
        for s in range(nb//st):
            a=s*st
            TA=A[a:a+st,:nb]; TW=A[a:a+st,nb:]
            B=[jnp.broadcast_to(TA[:,a+c:a+c+1],(st,nb)) for c in range(st)]
            D=jnp.zeros((st,nb),F)
            for c in range(st):
                piv=jnp.broadcast_to(B[c][c:c+1,:],(st,nb))
                D=jnp.where(sub==c,piv,D)
                if c<st-1:
                    m=jnp.where(sub>c,B[c]/piv,0.0)
                    for e in range(c+1,st):
                        B[e]=B[e]-m*B[e][c:c+1,:]
                    TA=TA-m*TA[c:c+1,:]
                    TW=TW-m*TW[c:c+1,:]
            q=lax.rsqrt(D)
            VA=TA*q; VW=TW*q
            A[a:a+st,:nb]=VA; A[a:a+st,nb:]=VW
            if s<nb//st-1:
                V=jnp.concatenate([VA,VW],axis=1)
                hi,mid,lo=split3(V)
                hi=hi.astype(F);mid=mid.astype(F);lo=lo.astype(F)
                L=jnp.concatenate([hi,hi,mid,hi,mid,lo],axis=0)[:,:nb].T.astype(BF)
                R=jnp.concatenate([hi,mid,hi,lo,mid,hi],axis=0).astype(BF)
                b=a+st
                A[b:,:]=A[b:,:]-lax.dot_general(L,R,(((1,),(0,)),((),())),preferred_element_type=F)[b:,:]
        out[o:o+nb,o:o+nb]=jnp.where(c_i<=r_i,A[:,:nb].T,0.0)
        if k<n//nb-1:
            out[o:o+nb,o+nb:]=jnp.zeros((nb,n-o-nb),F)
            W=jnp.where(c_i<=r_i,A[:,nb:],0.0)
            L21=lax.dot_general(S[o+nb:,o:o+nb],W,(((1,),(1,)),((),())),precision=lax.Precision.HIGHEST,preferred_element_type=F)
            out[o+nb:,o:o+nb]=L21
            S[o+nb:,o+nb:]=S[o+nb:,o+nb:]-lax.dot_general(L21,L21,(((1,),(1,)),((),())),precision=lax.Precision.HIGHEST,preferred_element_type=F)

CH = 256
PIECES = 4


def gram_add(G, b, T, R, ids):
    width = R.shape[1]
    M = jnp.where(ids == b, T, jnp.zeros((), T.dtype))
    at = 0
    for j in range(width // 256):
        o = 256 * j
        p = jnp.dot(M[o:, :], R[:, o : o + 256], preferred_element_type=F)
        h = width - o
        G[b, at : at + h, :] += p[:, :128]
        G[b, at + h : at + 2 * h - 128, :] += p[128:, 128:]
        at += 2 * h - 128


def exchange_kernel(doms, reps, cap, rows, eblk, lists, hblk, born, own_r, out,
                    TR, sbuf, rbuf, obuf, hob, G, RB, G2, RB2, OG, bpack, brecv,
                    ssem, rsem, hs, hr, bss, brs, xss, xrs, yss, yrs, oss, ors, lsem):
    p = lax.axis_index("dom")
    q = lax.axis_index("rep")
    me = p * reps + q
    total = doms * reps
    n_rows, width = rows.shape
    nch = sbuf.shape[0]
    cols = width // 128
    slab = cap * cols
    tri = G.shape[1]
    piece = tri // PIECES
    odd = p % 2
    mate = p + 1 - 2 * odd
    other = p - 1 + 2 * odd
    has_mate = mate < doms
    has_other = (other >= 0) & (other < doms)
    mesh_id = pl.DeviceIdType.MESH

    def halo_copy(ch):
        return pltpu.make_async_remote_copy(
            src_ref=sbuf.at[ch], dst_ref=rbuf.at[ch], send_sem=ssem.at[ch], recv_sem=rsem.at[ch],
            device_id={"dom": mate, "rep": q}, device_id_type=mesh_id)

    def ids_copy():
        return pltpu.make_async_remote_copy(
            src_ref=hblk.at[odd], dst_ref=hob, send_sem=hs, recv_sem=hr,
            device_id={"dom": other, "rep": q}, device_id_type=mesh_id)

    def owner_copy(i):
        at = pl.ds(i * piece, piece)
        return pltpu.make_async_remote_copy(
            src_ref=G2.at[q, at, :], dst_ref=OG.at[at, :], send_sem=oss.at[i], recv_sem=ors.at[i],
            device_id={"dom": other, "rep": q}, device_id_type=mesh_id)

    def stage(Gx, RBx, ss, rs, number):
        step, slot = 1, 0
        for _ in range(number):
            slot += reps // (2 * step)
            step *= 2
        bit = (q // step) % 2
        peer = q + step * (1 - 2 * bit)
        low = q % step
        made = []
        for i in range(reps // (2 * step)):
            away = low + (1 - bit) * step + 2 * step * i
            keep = low + bit * step + 2 * step * i
            for k in range(PIECES):
                at = pl.ds(k * piece, piece)
                n = (slot + i) * PIECES + k
                made.append((pltpu.make_async_remote_copy(
                    src_ref=Gx.at[away, at, :], dst_ref=RBx.at[slot + i, at, :],
                    send_sem=ss.at[n], recv_sem=rs.at[n],
                    device_id={"dom": p, "rep": peer}, device_id_type=mesh_id), keep, slot + i, k))
        return made

    stages = reps.bit_length() - 1

    def stage_start(Gx, RBx, ss, rs, number):
        for cp, _, _, _ in stage(Gx, RBx, ss, rs, number):
            cp.start()

    def stage_finish(Gx, RBx, ss, rs, number, then=None):
        for cp, keep, slot, k in stage(Gx, RBx, ss, rs, number):
            cp.wait_recv()
            at = pl.ds(k * piece, piece)
            Gx[keep, at, :] += RBx[slot, at, :]
            if then is not None:
                then(k)

    @pl.when(has_other)
    def _():
        ids_copy().start()

    for c in range(n_rows // CH):
        TR[:, c * CH : (c + 1) * CH] = rows[c * CH : (c + 1) * CH, :].T
    G2[...] = jnp.zeros_like(G2)

    def picked(half, ch):
        l = lists[:, pl.ds(pl.multiple_of((half * nch + ch) * CH, CH), CH)]
        i = lax.broadcasted_iota(jnp.int32, (n_rows, CH), 0)
        PT = jnp.where(i == l, 1.0, 0.0).astype(BF)
        return jnp.dot(TR[...], PT, preferred_element_type=F).astype(BF)

    def add_blocks(Gx, T, R, ids):
        def one(b, _):
            gram_add(Gx, b, T, R, ids)
            return 0
        lax.fori_loop(0, reps, one, 0)

    @pl.when(has_mate)
    def _():
        sbuf[0] = picked(1 - odd, 0)
        halo_copy(0).start()

    @pl.when(has_other)
    def _():
        ids_copy().wait_recv()

    def gather_step(ch, _):
        @pl.when(has_other)
        def _():
            obuf[...] = picked(odd, ch)
            T = obuf[...]
            add_blocks(G2, T, T.T, hob[:, pl.ds(pl.multiple_of(ch * CH, CH), CH)])

        @pl.when(has_mate & (ch < nch - 1))
        def _():
            sbuf[ch + 1] = picked(1 - odd, ch + 1)
            halo_copy(ch + 1).start()
        return 0

    lax.fori_loop(0, nch, gather_step, 0)

    @pl.when(has_other)
    def _():
        stage_start(G2, RB2, yss, yrs, 0)

    n_born = born.shape[0]
    ii = lax.broadcasted_iota(jnp.int32, (n_born, n_born), 0)
    jj = lax.broadcasted_iota(jnp.int32, (n_born, n_born), 1)
    own = jnp.broadcast_to(own_r[...].astype(F), (n_born, n_born))
    same = (own.T == own) & (ii < jj)
    rank = jnp.sum(jnp.where(same, 1.0, 0.0), axis=0, keepdims=True).astype(jnp.int32)
    base = own_r[...] * slab + rank * cols
    m = lax.broadcasted_iota(jnp.int32, (total * slab, n_born), 0)
    acc = jnp.zeros((total * slab, 128), F)
    for c in range(cols):
        oh = jnp.where(m == base + c, 1.0, 0.0).astype(BF)
        acc += jnp.dot(oh, born[:, c * 128 : (c + 1) * 128], preferred_element_type=F)
    bpack[...] = acc.astype(BF)

    def born_copy(to, frm):
        return pltpu.make_async_remote_copy(
            src_ref=bpack.at[pl.ds(pl.multiple_of(to * slab, slab), slab), :],
            dst_ref=brecv.at[pl.ds(pl.multiple_of(frm * slab, slab), slab), :],
            send_sem=bss.at[to], recv_sem=brs.at[frm],
            device_id={"dom": to // reps, "rep": to % reps}, device_id_type=mesh_id)

    def born_send(k, _):
        to = (me + k) % total
        born_copy(to, me).start()
        return 0

    lax.fori_loop(1, total, born_send, 0)
    mine = pl.ds(pl.multiple_of(me * slab, slab), slab)
    local = pltpu.make_async_copy(bpack.at[mine, :], brecv.at[mine, :], lsem)
    local.start()

    @pl.when(has_other)
    def _():
        for number in range(stages - 1):
            stage_finish(G2, RB2, yss, yrs, number)
            stage_start(G2, RB2, yss, yrs, number + 1)

    G[...] = jnp.zeros_like(G)

    def own_step(c, _):
        at = pl.ds(pl.multiple_of(c * CH, CH), CH)
        add_blocks(G, TR[:, at], rows[at, :], eblk[:, at])
        return 0

    lax.fori_loop(0, n_rows // CH, own_step, 0)

    def halo_step(ch, _):
        @pl.when(has_mate)
        def _():
            halo_copy(ch).wait_recv()
            T = rbuf[ch]
            add_blocks(G, T, T.T, hblk[1 - odd, :, pl.ds(pl.multiple_of(ch * CH, CH), CH)])
        return 0

    lax.fori_loop(0, nch, halo_step, 0)

    stage_start(G, RB, xss, xrs, 0)
    for number in range(stages - 1):
        stage_finish(G, RB, xss, xrs, number)
        stage_start(G, RB, xss, xrs, number + 1)

    @pl.when(has_other)
    def _():
        stage_finish(G2, RB2, yss, yrs, stages - 1, then=lambda k: owner_copy(k).start())

    def born_wait(k, _):
        frm = (me + k) % total
        born_copy(frm, frm).wait_recv()
        return 0

    lax.fori_loop(1, total, born_wait, 0)
    local.wait()
    n = total * cap
    mm = lax.broadcasted_iota(jnp.int32, (n, total * slab), 0)
    kk = lax.broadcasted_iota(jnp.int32, (n, total * slab), 1)
    Bv = brecv[...]
    V = jnp.concatenate(
        [jnp.dot(jnp.where(kk == mm * cols + c, 1.0, 0.0).astype(BF), Bv, preferred_element_type=F)
         for c in range(cols)], axis=1)
    VT = V.T.astype(BF)
    V = V.astype(BF)
    at = 0
    for j in range(width // 128):
        h = width - 128 * j
        out[at : at + h, :] = jnp.dot(
            VT[128 * j :, :], V[:, 128 * j : 128 * j + 128], preferred_element_type=F)
        at += h

    @pl.when(has_other)
    def _():
        for k in range(PIECES):
            owner_copy(k).wait_recv()
            at = pl.ds(k * piece, piece)
            out[at, :] += OG[at, :]

    for cp, _, slot, k in stage(G, RB, xss, xrs, stages - 1):
        cp.wait_recv()
        at = pl.ds(k * piece, piece)
        out[at, :] += G[q, at, :] + RB[slot, at, :]

    for number in range(stages):
        for cp, _, _, _ in stage(G, RB, xss, xrs, number):
            cp.wait_send()

    @pl.when(has_other)
    def _():
        ids_copy().wait_send()
        for number in range(stages):
            for cp, _, _, _ in stage(G2, RB2, yss, yrs, number):
                cp.wait_send()
        for k in range(PIECES):
            owner_copy(k).wait_send()

    def born_done(k, _):
        to = (me + k) % total
        born_copy(to, me).wait_send()
        return 0

    lax.fori_loop(1, total, born_done, 0)

    def halo_done(ch, _):
        @pl.when(has_mate)
        def _():
            halo_copy(ch).wait_send()
        return 0

    lax.fori_loop(0, nch, halo_done, 0)


def factor_kernel(packed, mass, out, S, A):
    width = S.shape[0]
    r_i = lax.broadcasted_iota(jnp.int32, (128, 128), 0)
    c_i = lax.broadcasted_iota(jnp.int32, (128, 128), 1)
    at = 0
    for j in range(width // 128):
        o = 128 * j
        h = width - o
        S[o:, o : o + 128] = packed[at : at + h, :] / width
        S[o : o + 128, o : o + 128] += jnp.where(r_i == c_i, mass[:, o : o + 128], 0.0)
        at += h
    chol_kernel(S, out, A)


def solution(mesh):
    doms, reps = mesh.shape["dom"], mesh.shape["rep"]
    total = doms * reps

    def local(elem_rows, elem_block, send_lists, halo_block, born_rows, born_owner, mass):
        n_rows, width = elem_rows.shape
        half = send_lists.shape[0] // 2
        nch = half // CH
        tri = (width // 128) * (width // 128 + 1) // 2 * 128
        slab = CAP * (width // 128)
        vm = pl.BlockSpec(memory_space=pltpu.VMEM)
        packed = pl.pallas_call(
            functools.partial(exchange_kernel, doms, reps, CAP),
            out_shape=jax.ShapeDtypeStruct((tri, 128), F),
            in_specs=[vm] * 6,
            out_specs=vm,
            scratch_shapes=[
                pltpu.VMEM((width, n_rows), BF),
                pltpu.VMEM((nch, width, CH), BF),
                pltpu.VMEM((nch, width, CH), BF),
                pltpu.VMEM((width, CH), BF),
                pltpu.VMEM((1, half), jnp.int32),
                pltpu.VMEM((reps, tri, 128), F),
                pltpu.VMEM((reps - 1, tri, 128), F),
                pltpu.VMEM((reps, tri, 128), F),
                pltpu.VMEM((reps - 1, tri, 128), F),
                pltpu.VMEM((tri, 128), F),
                pltpu.VMEM((total * slab, 128), BF),
                pltpu.VMEM((total * slab, 128), BF),
                pltpu.SemaphoreType.DMA((nch,)),
                pltpu.SemaphoreType.DMA((nch,)),
                pltpu.SemaphoreType.DMA,
                pltpu.SemaphoreType.DMA,
                pltpu.SemaphoreType.DMA((total,)),
                pltpu.SemaphoreType.DMA((total,)),
                pltpu.SemaphoreType.DMA(((reps - 1) * PIECES,)),
                pltpu.SemaphoreType.DMA(((reps - 1) * PIECES,)),
                pltpu.SemaphoreType.DMA(((reps - 1) * PIECES,)),
                pltpu.SemaphoreType.DMA(((reps - 1) * PIECES,)),
                pltpu.SemaphoreType.DMA((PIECES,)),
                pltpu.SemaphoreType.DMA((PIECES,)),
                pltpu.SemaphoreType.DMA,
            ],
            compiler_params=pltpu.CompilerParams(has_side_effects=True),
        )(elem_rows, elem_block[None, :], send_lists[None, :], halo_block.reshape(2, 1, half),
          born_rows, born_owner.reshape(1, -1))
        return pl.pallas_call(
            factor_kernel,
            out_shape=jax.ShapeDtypeStruct((width, width), F),
            in_specs=[vm] * 2,
            out_specs=vm,
            scratch_shapes=[pltpu.VMEM((width, width), F), pltpu.VMEM((128, 256), F)],
        )(packed, mass[None, :])

    both = P(("dom", "rep"))
    rows2 = P(("dom", "rep"), None)
    return jax.shard_map(local, mesh=mesh, in_specs=(rows2, both, both, both, rows2, rows2, both),
                         out_specs=rows2, check_vma=False)
```

```python
import functools

import jax
import jax.numpy as jnp
from jax import lax
from jax.experimental import pallas as pl
from jax.experimental.pallas import tpu as pltpu
from jax.sharding import PartitionSpec as P

CAP = 4
F=jnp.float32; BF=jnp.bfloat16

def split3(v):
    hi=v.astype(BF); r=v-hi.astype(F); mid=r.astype(BF); lo=(r-mid.astype(F)).astype(BF)
    return hi,mid,lo

def chol_kernel(S, out, A):
    n=S.shape[0]; nb=128; st=16
    for k in range(n//nb):
        o=k*nb
        r_i=lax.broadcasted_iota(jnp.int32,(nb,nb),0); c_i=lax.broadcasted_iota(jnp.int32,(nb,nb),1)
        A[:, :nb]=S[o:o+nb,o:o+nb]
        A[:, nb:]=jnp.where(r_i==c_i,1.0,0.0)
        sub=lax.broadcasted_iota(jnp.int32,(st,nb),0)
        for s in range(nb//st):
            a=s*st
            TA=A[a:a+st,:nb]; TW=A[a:a+st,nb:]
            B=[jnp.broadcast_to(TA[:,a+c:a+c+1],(st,nb)) for c in range(st)]
            D=jnp.zeros((st,nb),F)
            for c in range(st):
                piv=jnp.broadcast_to(B[c][c:c+1,:],(st,nb))
                D=jnp.where(sub==c,piv,D)
                if c<st-1:
                    m=jnp.where(sub>c,B[c]/piv,0.0)
                    for e in range(c+1,st):
                        B[e]=B[e]-m*B[e][c:c+1,:]
                    TA=TA-m*TA[c:c+1,:]
                    TW=TW-m*TW[c:c+1,:]
            q=lax.rsqrt(D)
            VA=TA*q; VW=TW*q
            A[a:a+st,:nb]=VA; A[a:a+st,nb:]=VW
            if s<nb//st-1:
                V=jnp.concatenate([VA,VW],axis=1)
                hi,mid,lo=split3(V)
                hi=hi.astype(F);mid=mid.astype(F);lo=lo.astype(F)
                L=jnp.concatenate([hi,hi,mid,hi,mid,lo],axis=0)[:,:nb].T.astype(BF)
                R=jnp.concatenate([hi,mid,hi,lo,mid,hi],axis=0).astype(BF)
                b=a+st
                A[b:,:]=A[b:,:]-lax.dot_general(L,R,(((1,),(0,)),((),())),preferred_element_type=F)[b:,:]
        out[o:o+nb,o:o+nb]=jnp.where(c_i<=r_i,A[:,:nb].T,0.0)
        if k<n//nb-1:
            out[o:o+nb,o+nb:]=jnp.zeros((nb,n-o-nb),F)
            W=jnp.where(c_i<=r_i,A[:,nb:],0.0)
            L21=lax.dot_general(S[o+nb:,o:o+nb],W,(((1,),(1,)),((),())),precision=lax.Precision.HIGHEST,preferred_element_type=F)
            out[o+nb:,o:o+nb]=L21
            S[o+nb:,o+nb:]=S[o+nb:,o+nb:]-lax.dot_general(L21,L21,(((1,),(1,)),((),())),precision=lax.Precision.HIGHEST,preferred_element_type=F)

CH = 256
PIECES = 4
OWN = 1024


def gram_add(G, T, R, ids):
    reps, width = G.shape[0], R.shape[1]
    M = [jnp.where(ids == b, T, jnp.zeros((), T.dtype)) for b in range(reps)]
    at = 0
    for j in range(width // 256):
        o = 256 * j
        h = width - o
        p = jnp.dot(jnp.concatenate([x[o:, :] for x in M], axis=0), R[:, o : o + 256],
                    preferred_element_type=F)
        for b in range(reps):
            G[b, at : at + h, :] += p[b * h : (b + 1) * h, :128]
            G[b, at + h : at + 2 * h - 128, :] += p[b * h + 128 : (b + 1) * h, 128:]
        at += 2 * h - 128


def exchange_kernel(doms, reps, cap, rows, eblk, lists, hblk, born, own_r, out,
                    TR, sbuf, rbuf, obuf, hob, G, RB, G2, RB2, OG, bpack, brecv,
                    ssem, rsem, hs, hr, bss, brs, xss, xrs, yss, yrs, oss, ors, lsem):
    p = lax.axis_index("dom")
    q = lax.axis_index("rep")
    me = p * reps + q
    total = doms * reps
    n_rows, width = rows.shape
    nch = sbuf.shape[0]
    cols = width // 128
    slab = cap * cols
    tri = G.shape[1]
    piece = tri // PIECES
    odd = p % 2
    mate = p + 1 - 2 * odd
    other = p - 1 + 2 * odd
    has_mate = mate < doms
    has_other = (other >= 0) & (other < doms)
    mesh_id = pl.DeviceIdType.MESH

    def halo_copy(ch):
        return pltpu.make_async_remote_copy(
            src_ref=sbuf.at[ch], dst_ref=rbuf.at[ch], send_sem=ssem.at[ch], recv_sem=rsem.at[ch],
            device_id={"dom": mate, "rep": q}, device_id_type=mesh_id)

    def ids_copy():
        return pltpu.make_async_remote_copy(
            src_ref=hblk.at[odd], dst_ref=hob, send_sem=hs, recv_sem=hr,
            device_id={"dom": other, "rep": q}, device_id_type=mesh_id)

    def owner_copy(i):
        at = pl.ds(i * piece, piece)
        return pltpu.make_async_remote_copy(
            src_ref=G2.at[q, at, :], dst_ref=OG.at[at, :], send_sem=oss.at[i], recv_sem=ors.at[i],
            device_id={"dom": other, "rep": q}, device_id_type=mesh_id)

    def stage(Gx, RBx, ss, rs, number):
        step, slot = 1, 0
        for _ in range(number):
            slot += reps // (2 * step)
            step *= 2
        bit = (q // step) % 2
        peer = q + step * (1 - 2 * bit)
        low = q % step
        made = []
        for i in range(reps // (2 * step)):
            away = low + (1 - bit) * step + 2 * step * i
            keep = low + bit * step + 2 * step * i
            for k in range(PIECES):
                at = pl.ds(k * piece, piece)
                n = (slot + i) * PIECES + k
                made.append((pltpu.make_async_remote_copy(
                    src_ref=Gx.at[away, at, :], dst_ref=RBx.at[slot + i, at, :],
                    send_sem=ss.at[n], recv_sem=rs.at[n],
                    device_id={"dom": p, "rep": peer}, device_id_type=mesh_id), keep, slot + i, k))
        return made

    stages = reps.bit_length() - 1

    def stage_start(Gx, RBx, ss, rs, number):
        for cp, _, _, _ in stage(Gx, RBx, ss, rs, number):
            cp.start()

    def stage_finish(Gx, RBx, ss, rs, number, then=None):
        for cp, keep, slot, k in stage(Gx, RBx, ss, rs, number):
            cp.wait_recv()
            at = pl.ds(k * piece, piece)
            Gx[keep, at, :] += RBx[slot, at, :]
            if then is not None:
                then(k)

    @pl.when(has_other)
    def _():
        ids_copy().start()

    for c in range(n_rows // CH):
        TR[:, c * CH : (c + 1) * CH] = rows[c * CH : (c + 1) * CH, :].T
    G2[...] = jnp.zeros_like(G2)

    def picked(half, ch):
        l = lists[:, pl.ds(pl.multiple_of((half * nch + ch) * CH, CH), CH)]
        i = lax.broadcasted_iota(jnp.int32, (n_rows, CH), 0)
        PT = jnp.where(i == l, 1.0, 0.0).astype(BF)
        return jnp.dot(TR[...], PT, preferred_element_type=F).astype(BF)

    def add_blocks(Gx, T, R, ids):
        gram_add(Gx, T, R, ids)

    @pl.when(has_mate)
    def _():
        sbuf[0] = picked(1 - odd, 0)
        halo_copy(0).start()

    @pl.when(has_other)
    def _():
        ids_copy().wait_recv()

    def gather_step(ch, _):
        @pl.when(has_other)
        def _():
            obuf[...] = picked(odd, ch)
            T = obuf[...]
            add_blocks(G2, T, T.T, hob[:, pl.ds(pl.multiple_of(ch * CH, CH), CH)])

        @pl.when(has_mate & (ch < nch - 1))
        def _():
            sbuf[ch + 1] = picked(1 - odd, ch + 1)
            halo_copy(ch + 1).start()
        return 0

    lax.fori_loop(0, nch, gather_step, 0)

    @pl.when(has_other)
    def _():
        stage_start(G2, RB2, yss, yrs, 0)

    n_born = born.shape[0]
    ii = lax.broadcasted_iota(jnp.int32, (n_born, n_born), 0)
    jj = lax.broadcasted_iota(jnp.int32, (n_born, n_born), 1)
    own = jnp.broadcast_to(own_r[...].astype(F), (n_born, n_born))
    same = (own.T == own) & (ii < jj)
    rank = jnp.sum(jnp.where(same, 1.0, 0.0), axis=0, keepdims=True).astype(jnp.int32)
    base = own_r[...] * slab + rank * cols
    m = lax.broadcasted_iota(jnp.int32, (total * slab, n_born), 0)
    acc = jnp.zeros((total * slab, 128), F)
    for c in range(cols):
        oh = jnp.where(m == base + c, 1.0, 0.0).astype(BF)
        acc += jnp.dot(oh, born[:, c * 128 : (c + 1) * 128], preferred_element_type=F)
    bpack[...] = acc.astype(BF)

    def born_copy(to, frm):
        return pltpu.make_async_remote_copy(
            src_ref=bpack.at[pl.ds(pl.multiple_of(to * slab, slab), slab), :],
            dst_ref=brecv.at[pl.ds(pl.multiple_of(frm * slab, slab), slab), :],
            send_sem=bss.at[to], recv_sem=brs.at[frm],
            device_id={"dom": to // reps, "rep": to % reps}, device_id_type=mesh_id)

    def born_send(k, _):
        to = (me + k) % total
        born_copy(to, me).start()
        return 0

    lax.fori_loop(1, total, born_send, 0)
    mine = pl.ds(pl.multiple_of(me * slab, slab), slab)
    local = pltpu.make_async_copy(bpack.at[mine, :], brecv.at[mine, :], lsem)
    local.start()

    @pl.when(has_other)
    def _():
        for number in range(stages - 1):
            stage_finish(G2, RB2, yss, yrs, number)
            stage_start(G2, RB2, yss, yrs, number + 1)

    G[...] = jnp.zeros_like(G)

    def own_step(c, _):
        at = pl.ds(pl.multiple_of(c * OWN, OWN), OWN)
        add_blocks(G, TR[:, at], rows[at, :], eblk[:, at])
        return 0

    lax.fori_loop(0, n_rows // OWN, own_step, 0)

    def halo_step(ch, _):
        @pl.when(has_mate)
        def _():
            halo_copy(ch).wait_recv()
            T = rbuf[ch]
            add_blocks(G, T, T.T, hblk[1 - odd, :, pl.ds(pl.multiple_of(ch * CH, CH), CH)])
        return 0

    lax.fori_loop(0, nch, halo_step, 0)

    stage_start(G, RB, xss, xrs, 0)
    for number in range(stages - 1):
        stage_finish(G, RB, xss, xrs, number)
        stage_start(G, RB, xss, xrs, number + 1)

    @pl.when(has_other)
    def _():
        stage_finish(G2, RB2, yss, yrs, stages - 1, then=lambda k: owner_copy(k).start())

    def born_wait(k, _):
        frm = (me + k) % total
        born_copy(frm, frm).wait_recv()
        return 0

    lax.fori_loop(1, total, born_wait, 0)
    local.wait()
    n = total * cap
    mm = lax.broadcasted_iota(jnp.int32, (n, total * slab), 0)
    kk = lax.broadcasted_iota(jnp.int32, (n, total * slab), 1)
    Bv = brecv[...]
    V = jnp.concatenate(
        [jnp.dot(jnp.where(kk == mm * cols + c, 1.0, 0.0).astype(BF), Bv, preferred_element_type=F)
         for c in range(cols)], axis=1)
    VT = V.T.astype(BF)
    V = V.astype(BF)
    at = 0
    for j in range(width // 128):
        h = width - 128 * j
        out[at : at + h, :] = jnp.dot(
            VT[128 * j :, :], V[:, 128 * j : 128 * j + 128], preferred_element_type=F)
        at += h

    @pl.when(has_other)
    def _():
        for k in range(PIECES):
            owner_copy(k).wait_recv()
            at = pl.ds(k * piece, piece)
            out[at, :] += OG[at, :]

    for cp, _, slot, k in stage(G, RB, xss, xrs, stages - 1):
        cp.wait_recv()
        at = pl.ds(k * piece, piece)
        out[at, :] += G[q, at, :] + RB[slot, at, :]

    for number in range(stages):
        for cp, _, _, _ in stage(G, RB, xss, xrs, number):
            cp.wait_send()

    @pl.when(has_other)
    def _():
        ids_copy().wait_send()
        for number in range(stages):
            for cp, _, _, _ in stage(G2, RB2, yss, yrs, number):
                cp.wait_send()
        for k in range(PIECES):
            owner_copy(k).wait_send()

    def born_done(k, _):
        to = (me + k) % total
        born_copy(to, me).wait_send()
        return 0

    lax.fori_loop(1, total, born_done, 0)

    def halo_done(ch, _):
        @pl.when(has_mate)
        def _():
            halo_copy(ch).wait_send()
        return 0

    lax.fori_loop(0, nch, halo_done, 0)


def factor_kernel(packed, mass, out, S, A):
    width = S.shape[0]
    r_i = lax.broadcasted_iota(jnp.int32, (128, 128), 0)
    c_i = lax.broadcasted_iota(jnp.int32, (128, 128), 1)
    at = 0
    for j in range(width // 128):
        o = 128 * j
        h = width - o
        S[o:, o : o + 128] = packed[at : at + h, :] / width
        S[o : o + 128, o : o + 128] += jnp.where(r_i == c_i, mass[:, o : o + 128], 0.0)
        at += h
    chol_kernel(S, out, A)


def solution(mesh):
    doms, reps = mesh.shape["dom"], mesh.shape["rep"]
    total = doms * reps

    def local(elem_rows, elem_block, send_lists, halo_block, born_rows, born_owner, mass):
        n_rows, width = elem_rows.shape
        half = send_lists.shape[0] // 2
        nch = half // CH
        tri = (width // 128) * (width // 128 + 1) // 2 * 128
        slab = CAP * (width // 128)
        vm = pl.BlockSpec(memory_space=pltpu.VMEM)
        packed = pl.pallas_call(
            functools.partial(exchange_kernel, doms, reps, CAP),
            out_shape=jax.ShapeDtypeStruct((tri, 128), F),
            in_specs=[vm] * 6,
            out_specs=vm,
            scratch_shapes=[
                pltpu.VMEM((width, n_rows), BF),
                pltpu.VMEM((nch, width, CH), BF),
                pltpu.VMEM((nch, width, CH), BF),
                pltpu.VMEM((width, CH), BF),
                pltpu.VMEM((1, half), jnp.int32),
                pltpu.VMEM((reps, tri, 128), F),
                pltpu.VMEM((reps - 1, tri, 128), F),
                pltpu.VMEM((reps, tri, 128), F),
                pltpu.VMEM((reps - 1, tri, 128), F),
                pltpu.VMEM((tri, 128), F),
                pltpu.VMEM((total * slab, 128), BF),
                pltpu.VMEM((total * slab, 128), BF),
                pltpu.SemaphoreType.DMA((nch,)),
                pltpu.SemaphoreType.DMA((nch,)),
                pltpu.SemaphoreType.DMA,
                pltpu.SemaphoreType.DMA,
                pltpu.SemaphoreType.DMA((total,)),
                pltpu.SemaphoreType.DMA((total,)),
                pltpu.SemaphoreType.DMA(((reps - 1) * PIECES,)),
                pltpu.SemaphoreType.DMA(((reps - 1) * PIECES,)),
                pltpu.SemaphoreType.DMA(((reps - 1) * PIECES,)),
                pltpu.SemaphoreType.DMA(((reps - 1) * PIECES,)),
                pltpu.SemaphoreType.DMA((PIECES,)),
                pltpu.SemaphoreType.DMA((PIECES,)),
                pltpu.SemaphoreType.DMA,
            ],
            compiler_params=pltpu.CompilerParams(has_side_effects=True),
        )(elem_rows, elem_block[None, :], send_lists[None, :], halo_block.reshape(2, 1, half),
          born_rows, born_owner.reshape(1, -1))
        return pl.pallas_call(
            factor_kernel,
            out_shape=jax.ShapeDtypeStruct((width, width), F),
            in_specs=[vm] * 2,
            out_specs=vm,
            scratch_shapes=[pltpu.VMEM((width, width), F), pltpu.VMEM((128, 256), F)],
        )(packed, mass[None, :])

    both = P(("dom", "rep"))
    rows2 = P(("dom", "rep"), None)
    return jax.shard_map(local, mesh=mesh, in_specs=(rows2, both, both, both, rows2, rows2, both),
                         out_specs=rows2, check_vma=False)
```
